32 devices in a mesh: groups: 2 (over y), ctx: 16 (over z, x, core).
Axes of the slice: x: 2, y: 2, z: 4, core: 2. Of those that a mesh axis runs over, the one named last changes fastest.
Arguments:
- queries: bfloat16 [4096, 4096], P(('groups', 'ctx')), parts along dimension 0, may hold values from -12 to 12
- context_keys: bfloat16 [32, 2048, 512], P('groups', 'ctx'), parts along dimension 0, may hold values from -6 to 6
- context_values: bfloat16 [32, 2048, 512], P('groups', 'ctx'), parts along dimension 0, may hold values from -6 to 6
- forward_output: bfloat16 [4096, 4096], P(('groups', 'ctx')), parts along dimension 0, may hold values from -6 to 6
- output_cotangent: bfloat16 [4096, 4096], P(('groups', 'ctx')), parts along dimension 0, may hold values from -48 to 48
- verticals: int32 [8, 8], P('groups'), parts along dimension 0, may hold values from 0 to 511, as said below
- offsets: int32 [8, 3], P('groups'), parts along dimension 0, may hold values from 1 to 10, as said below
- slab_index: int32 [2], P('groups'), parts along dimension 0, may hold values from 1 to 15
Outputs:
- query_grad: bfloat16 [4096, 4096], P(('groups', 'ctx')), parts along dimension 0
- key_gradient: bfloat16 [32, 2048, 512], P('groups', 'ctx'), parts along dimension 0
- value_gradient: bfloat16 [32, 2048, 512], P('groups', 'ctx'), parts along dimension 0
The draws below stay inside these ranges and needn't reach their ends.
There are 2 independent parts, one for each index of `groups`. The reference program is written for one: setup_inputs(seed, part) draws one part's arguments, and reference() takes and returns one part's arrays. A program takes and returns all parts, laid end to end along the dimension named above; each array names one. Nothing has to cross between parts.
Inputs may be any that keep to these rules, and one draw needn't show every extreme that they name: `verticals`: each row holds 8 distinct block numbers; the first of every row is 0, and some row names the last block. Each row holds 3 distinct offsets; some row names 10.
All inputs are finite; a program needn't handle non-finite values.
Results may differ from the reference program's by a relative error of at most 0.0051.
Values may be sent and summed in bfloat16 or wider, within the bound.
A program may use at most 128 MiB of HBM per device.

```python
import math
import jax
import jax.numpy as jnp
from jax import lax

HEAD_SIZE = 128
QUERY_HEADS = 32
KEY_VALUE_HEADS = 4
MASK_BLOCK_SIZE = 64
SLAB_COUNT = 16
SLASH_RANGE = 11
NV = 8
SLASH_COUNT = 3
SLAB_QUERY_ROWS = 2048


def draw_queries(key, part):
    random_seed_key = jax.random.fold_in(key, 5)
    unmasked_rows = jnp.clip(jax.random.normal(random_seed_key, (SLAB_QUERY_ROWS, QUERY_HEADS * HEAD_SIZE), jnp.float32), -6.0, 6.0)
    return unmasked_rows.astype(jnp.bfloat16)


def draw_context_keys(key, part):
    random_seed_key = jax.random.fold_in(key, 6)
    unmasked_rows = jnp.clip(jax.random.normal(random_seed_key, (SLAB_COUNT, SLAB_QUERY_ROWS, KEY_VALUE_HEADS * HEAD_SIZE), jnp.float32), -6.0, 6.0)
    return unmasked_rows.astype(jnp.bfloat16)


def draw_verticals(key, part):
    block_count_all = SLAB_COUNT * SLAB_QUERY_ROWS // MASK_BLOCK_SIZE
    per_head_seeds = jax.random.split(jax.random.fold_in(key, 9), KEY_VALUE_HEADS)

    def one_head(head_key):
        shuffled = jax.random.permutation(head_key, block_count_all - 2) + 1
        return shuffled[:NV - 1]
    remaining_slabs = jax.vmap(one_head)(per_head_seeds).astype(jnp.int32)
    selected_blocks = jax.random.randint(jax.random.fold_in(key, 10), (), 0, KEY_VALUE_HEADS)
    remaining_slabs = remaining_slabs.at[:, 0].set(jnp.where(jnp.arange(KEY_VALUE_HEADS) == selected_blocks, block_count_all - 1, remaining_slabs[:, 0]).astype(jnp.int32))
    return jnp.concatenate([jnp.zeros((KEY_VALUE_HEADS, 1), jnp.int32), remaining_slabs], axis=1).astype(jnp.int32)


def draw_offsets(key, part):
    per_head_seeds = jax.random.split(jax.random.fold_in(key, 21), KEY_VALUE_HEADS)

    def one_head(head_key):
        shuffled = jax.random.permutation(head_key, SLASH_RANGE - 2) + 1
        return shuffled[:SLASH_COUNT]
    chosen_rows = jax.vmap(one_head)(per_head_seeds).astype(jnp.int32)
    farthest_head = jax.random.randint(jax.random.fold_in(key, 22), (), 0, KEY_VALUE_HEADS)
    chosen_rows = chosen_rows.at[:, 0].set(jnp.where(jnp.arange(KEY_VALUE_HEADS) == farthest_head, SLASH_RANGE - 1, chosen_rows[:, 0]).astype(jnp.int32))
    return chosen_rows.astype(jnp.int32)


def level_of(rng, dims, cuts, least, high):
    level = 1.0
    for position, parts in cuts:
        steps = jax.random.uniform(jax.random.fold_in(jax.random.fold_in(rng, 6), position), (parts,), jnp.float32, least / len(cuts), high / len(cuts))
        level = level * jnp.repeat(jnp.exp(steps), dims[position] // parts).reshape((-1,) + (1,) * (len(dims) - 1 - position))
    return level


def gaussian(rng, dims, deviation, reach, cuts=(), held_as=jnp.bfloat16):
    factor_of = level_of(rng, dims, cuts, -0.22, 0.18) if cuts else 1.0
    values = jax.random.normal(rng, dims, jnp.float32) * deviation * factor_of
    return jnp.minimum(jnp.maximum(values, -reach), reach).astype(held_as)


def setup_inputs(seed: int = 0, part: int = 0) -> dict:
    key_of = jax.random.split(jax.random.key(seed), 9)
    part_splits = jax.random.split(jax.random.fold_in(key_of[8], part), 9)
    queries = draw_queries(jax.random.fold_in(jax.random.fold_in(key_of[8], part), 71), part)
    context_keys = draw_context_keys(jax.random.fold_in(jax.random.fold_in(key_of[8], part), 71), part)
    context_values = gaussian(part_splits[2], (SLAB_COUNT, SLAB_QUERY_ROWS, KEY_VALUE_HEADS * HEAD_SIZE), 1.0, 6.0, ((1, 16),))
    forward_output = gaussian(part_splits[3], (SLAB_QUERY_ROWS, QUERY_HEADS * HEAD_SIZE), 1.0, 6.0, ((0, 16),))
    output_cotangent = gaussian(part_splits[4], (SLAB_QUERY_ROWS, QUERY_HEADS * HEAD_SIZE), 8.0, 48.0, ((0, 16),))
    verticals = draw_verticals(jax.random.fold_in(jax.random.fold_in(key_of[8], part), 71), part)
    offsets = draw_offsets(jax.random.fold_in(jax.random.fold_in(key_of[8], part), 71), part)
    slab_index = jax.random.randint(part_splits[7], (1,), 1, SLAB_COUNT).astype(jnp.int32)
    return dict(queries=queries, context_keys=context_keys, context_values=context_values, forward_output=forward_output, output_cotangent=output_cotangent, verticals=verticals, offsets=offsets, slab_index=slab_index)


def lowered(source):
    return lax.optimization_barrier(source.astype(jnp.bfloat16)).astype(jnp.float32)

def reference(queries, context_keys, context_values, forward_output, output_cotangent, verticals, offsets, slab_index):
    query_per_key_head = QUERY_HEADS // KEY_VALUE_HEADS
    blocks_per_slab = SLAB_QUERY_ROWS // MASK_BLOCK_SIZE
    context_blocks = SLAB_COUNT * blocks_per_slab
    scaling = 1.0 / math.sqrt(HEAD_SIZE)
    first_block = (slab_index[0] * blocks_per_slab).astype(jnp.int32)
    key_pieces = context_keys.reshape(context_blocks, MASK_BLOCK_SIZE, KEY_VALUE_HEADS, HEAD_SIZE).transpose(2, 0, 1, 3)
    value_pieces = context_values.reshape(context_blocks, MASK_BLOCK_SIZE, KEY_VALUE_HEADS, HEAD_SIZE).transpose(2, 0, 1, 3)
    query_pieces = queries.reshape(blocks_per_slab, MASK_BLOCK_SIZE, KEY_VALUE_HEADS, query_per_key_head, HEAD_SIZE)
    gradient_pieces = output_cotangent.reshape(blocks_per_slab, MASK_BLOCK_SIZE, KEY_VALUE_HEADS, query_per_key_head, HEAD_SIZE)
    output_pieces = forward_output.reshape(blocks_per_slab, MASK_BLOCK_SIZE, KEY_VALUE_HEADS, query_per_key_head, HEAD_SIZE)
    head_numbers = jnp.arange(KEY_VALUE_HEADS, dtype=jnp.int32)[:, None]
    lower_tri = jnp.arange(MASK_BLOCK_SIZE)[:, None] >= jnp.arange(MASK_BLOCK_SIZE)[None, :]
    zero_gradients = jnp.zeros((KEY_VALUE_HEADS, context_blocks, MASK_BLOCK_SIZE, HEAD_SIZE), jnp.float32)

    def one_block(running, block_index):
        key_gradient_sum, value_gradient_sum = running
        present_slab = first_block + block_index
        slash_blocks = (present_slab - offsets).astype(jnp.int32)
        collide = jnp.any(slash_blocks[:, :, None] == verticals[:, None, :], axis=2)
        slash_valid = (offsets > 0) & jnp.logical_not(collide)
        vertical_valid = verticals < present_slab
        diagonal_mask = jnp.zeros((KEY_VALUE_HEADS, 1), jnp.int32) + present_slab
        cand_blocks = jnp.concatenate([diagonal_mask, verticals.astype(jnp.int32), slash_blocks], axis=1).astype(jnp.int32)
        candidate_valid = jnp.concatenate([jnp.ones((KEY_VALUE_HEADS, 1), jnp.bool_), vertical_valid, slash_valid], axis=1)
        cand_keys = key_pieces[head_numbers, cand_blocks].astype(jnp.float32)
        cand_values = value_pieces[head_numbers, cand_blocks].astype(jnp.float32)
        causal = (cand_blocks < present_slab)[:, None, :, None] | lower_tri[None, :, None, :]
        visible = candidate_valid[:, None, :, None] & causal
        q_block = lax.dynamic_index_in_dim(query_pieces, block_index, 0, keepdims=False).astype(jnp.float32)
        grad_block = lax.dynamic_index_in_dim(gradient_pieces, block_index, 0, keepdims=False).astype(jnp.float32)
        out_block = lax.dynamic_index_in_dim(output_pieces, block_index, 0, keepdims=False).astype(jnp.float32)
        scores = jnp.einsum('rhgd,hctd->hrgct', q_block, cand_keys) * scaling
        masked = jnp.where(visible[:, :, None], scores, -jnp.inf)
        row_max = lax.optimization_barrier(jnp.max(masked, axis=(3, 4), keepdims=True))
        row_sum = lax.optimization_barrier(jnp.sum(jnp.exp(masked - row_max), axis=(3, 4), keepdims=True))
        weights = jnp.exp(masked - (row_max + jnp.log(row_sum)))
        delta_rows = lax.optimization_barrier(jnp.sum(grad_block * out_block, axis=-1))
        weight_grad = jnp.einsum('rhgd,hctd->hrgct', grad_block, cand_values)
        score_grad = weights * (weight_grad - jnp.transpose(delta_rows, (1, 0, 2))[:, :, :, None, None])
        weights_low = lowered(weights)
        score_low = lowered(score_grad)
        value_part = jnp.einsum('hrgct,rhgd->hctd', weights_low, grad_block)
        key_part = jnp.einsum('hrgct,rhgd->hctd', score_low, q_block) * scaling
        query_part = jnp.einsum('hrgct,hctd->rhgd', score_low, cand_keys) * scaling
        key_gradient_sum = key_gradient_sum.at[head_numbers, cand_blocks].add(key_part)
        value_gradient_sum = value_gradient_sum.at[head_numbers, cand_blocks].add(value_part)
        return ((key_gradient_sum, value_gradient_sum), query_part)
    (key_gradient_sum, value_gradient_sum), query_parts = lax.scan(one_block, (zero_gradients, zero_gradients), jnp.arange(blocks_per_slab, dtype=jnp.int32))
    query_grad = query_parts.reshape(SLAB_QUERY_ROWS, QUERY_HEADS * HEAD_SIZE).astype(jnp.bfloat16)
    key_gradient = key_gradient_sum.transpose(1, 2, 0, 3).reshape(SLAB_COUNT, SLAB_QUERY_ROWS, KEY_VALUE_HEADS * HEAD_SIZE).astype(jnp.bfloat16)
    value_gradient = value_gradient_sum.transpose(1, 2, 0, 3).reshape(SLAB_COUNT, SLAB_QUERY_ROWS, KEY_VALUE_HEADS * HEAD_SIZE).astype(jnp.bfloat16)
    return (query_grad, key_gradient, value_gradient)
```

```python
import functools
import math

import jax
import jax.numpy as jnp
from jax import lax
from jax.experimental import pallas as pl
from jax.experimental.pallas import tpu as pltpu
from jax.sharding import PartitionSpec as P

BLOCK = 64
WDEV = 5
NV = 8
SLASH_COUNT = 3
NEG = -1e30
LIMIT = 48 * 1024 * 1024
MESH = pl.DeviceIdType.MESH


def pick_kernel(per_device, devices, me_ref, slab_ref, vert_ref, ck, cv, pk, src, pick_sem, src_sem):
    me = me_ref[0]
    slab = slab_ref[0]
    heads = vert_ref.shape[0]
    dim = ck.shape[2] // heads
    copies = []
    for which in range(2):
        for kind, ref in enumerate((ck, cv)):
            copy = pltpu.make_async_copy(
                ref.at[slab - which], src.at[which, kind], src_sem.at[which, kind]
            )
            copy.start()
            copies.append(copy)
    pk[...] = jnp.zeros_like(pk)

    def owned_copies(h, v):
        block = vert_ref[h, v]
        region = block // (per_device * devices)
        inner = block % (per_device * devices)
        start = pl.multiple_of((inner % per_device) * BLOCK, BLOCK)
        mine = inner // per_device == me
        made = [
            pltpu.make_async_copy(
                ref.at[region, pl.ds(start, BLOCK), pl.ds(h * dim, dim)],
                pk.at[h * NV + v, kind],
                pick_sem.at[h * NV + v, kind],
            )
            for kind, ref in enumerate((ck, cv))
        ]
        return mine, made

    for h in range(heads):
        for v in range(NV):
            mine, made = owned_copies(h, v)

            @pl.when(mine)
            def _():
                for copy in made:
                    copy.start()

    for copy in copies:
        copy.wait()
    for h in range(heads):
        for v in range(NV):
            mine, made = owned_copies(h, v)

            @pl.when(mine)
            def _():
                for copy in made:
                    copy.wait()


def add_rows(target, target_at, parts, count):
    step = min(count, 64)

    def one(i, carry):
        at = pl.multiple_of(i * step, step)
        total = None
        for ref, start in parts:
            rows = ref[pl.ds(pl.multiple_of(start + at, step), step), :].astype(jnp.float32)
            total = rows if total is None else total + rows
        target[pl.ds(pl.multiple_of(target_at + at, step), step), :] = total.astype(target.dtype)
        return carry

    lax.fori_loop(0, count // step, one, 0)


def exchange_kernel(
    devices,
    back,
    src,
    vert,
    win,
    out,
    got1,
    got2,
    got3,
    sum1,
    sum2,
    win_send,
    win_recv,
    own_sem,
    send,
    recv,
    far_send,
    far_recv,
    gather_send,
    gather_recv,
):
    me = lax.axis_index("ctx")
    rows = vert.shape[0]
    half, quarter = rows // 2, rows // 4
    far = devices // 4
    piece = rows // devices
    c, x, z = me % 2, (me // 2) % 2, me // 4
    core_peer = me + 1 - 2 * c
    x_peer = me + 2 - 4 * x

    barrier = pltpu.get_barrier_semaphore()

    def greet(k, carry):
        pl.semaphore_signal(
            barrier, inc=1, device_id={"ctx": (me + k) % devices}, device_id_type=MESH
        )
        return carry

    lax.fori_loop(1, devices, greet, 0)
    pl.semaphore_wait(barrier, devices - 1)

    def remote(a, b, s, r, peer):
        return pltpu.make_async_remote_copy(
            src_ref=a, dst_ref=b, send_sem=s, recv_sem=r, device_id={"ctx": peer}, device_id_type=MESH
        )

    def at(ref, start, count):
        return ref.at[pl.ds(pl.multiple_of(start, count), count)]

    first = remote(at(vert, (1 - c) * half, half), got1, send.at[0], recv.at[0], core_peer)
    first.start()
    window = []
    for d in range(1, WDEV + 1):
        if back:
            copy = remote(
                src.at[WDEV - d],
                win.at[d - 1],
                win_send.at[d - 1],
                win_recv.at[d - 1],
                (me + devices - d) % devices,
            )
        else:
            copy = remote(
                src.at[(me + d) // devices],
                win.at[WDEV - d],
                win_send.at[d - 1],
                win_recv.at[d - 1],
                (me + d) % devices,
            )
        window.append(copy)
    own = None
    if not back:
        own = pltpu.make_async_copy(src.at[0], win.at[WDEV], own_sem.at[0])
        own.start()
    first.wait()
    for copy in window:
        copy.start()
    add_rows(sum1, 0, [(vert, c * half), (got1, 0)], half)
    second = remote(at(sum1, (1 - x) * quarter, quarter), got2, send.at[1], recv.at[1], x_peer)
    second.start()
    second.wait()
    add_rows(sum2, 0, [(sum1, x * quarter), (got2, 0)], quarter)
    spread = []
    for k in range(1, far):
        peer_z = (z + k) % far
        copy = remote(
            at(sum2, peer_z * piece, piece),
            got3.at[pl.ds((k - 1) * piece, piece)],
            far_send.at[k - 1],
            far_recv.at[k - 1],
            peer_z * 4 + me % 4,
        )
        copy.start()
        spread.append(copy)
    for copy in spread:
        copy.wait()
    base = c * half + x * quarter + z * piece
    add_rows(
        out, base, [(sum2, z * piece)] + [(got3, k * piece) for k in range(far - 1)], piece
    )
    gathered = []
    for k in range(1, far):
        peer_z = (z + k) % far
        copy = remote(
            at(out, base, piece),
            at(out, base, piece),
            gather_send.at[k - 1],
            gather_recv.at[k - 1],
            peer_z * 4 + me % 4,
        )
        copy.start()
        gathered.append(copy)
    for copy in gathered:
        copy.wait()
    third = remote(
        at(out, c * half + x * quarter, quarter),
        at(out, c * half + x * quarter, quarter),
        send.at[2],
        recv.at[2],
        x_peer,
    )
    third.start()
    third.wait()
    fourth = remote(at(out, c * half, half), at(out, c * half, half), send.at[3], recv.at[3], core_peer)
    fourth.start()
    fourth.wait()
    if own is not None:
        own.wait()
    for copy in window:
        copy.wait()


def exchange(src, vert, devices, back):
    rows, dim = vert.shape
    far = devices // 4
    piece = rows // devices
    slots = WDEV if back else WDEV + 1
    dma = pltpu.SemaphoreType.DMA
    return pl.pallas_call(
        functools.partial(exchange_kernel, devices, back),
        out_shape=(
            jax.ShapeDtypeStruct((slots,) + src.shape[1:], jnp.bfloat16),
            jax.ShapeDtypeStruct((rows, dim), jnp.bfloat16),
        ),
        in_specs=[
            pl.BlockSpec(memory_space=pl.ANY),
            pl.BlockSpec(memory_space=pltpu.VMEM),
        ],
        out_specs=(
            pl.BlockSpec(memory_space=pl.ANY),
            pl.BlockSpec(memory_space=pltpu.VMEM),
        ),
        scratch_shapes=[
            pltpu.VMEM((rows // 2, dim), jnp.bfloat16),
            pltpu.VMEM((rows // 4, dim), jnp.bfloat16),
            pltpu.VMEM(((far - 1) * piece, dim), jnp.bfloat16),
            pltpu.VMEM((rows // 2, dim), jnp.bfloat16),
            pltpu.VMEM((rows // 4, dim), jnp.bfloat16),
            dma((WDEV,)),
            dma((WDEV,)),
            dma((1,)),
            dma((4,)),
            dma((4,)),
            dma((far - 1,)),
            dma((far - 1,)),
            dma((far - 1,)),
            dma((far - 1,)),
        ],
        compiler_params=pltpu.CompilerParams(
            collective_id=1 if back else 0, has_side_effects=True, vmem_limit_bytes=LIMIT
        ),
        name="send_back" if back else "send_out",
    )(src, vert)


def attend_kernel(
    per_device,
    first_ref,
    vert_ref,
    off_ref,
    q_ref,
    g_ref,
    f_ref,
    win_ref,
    vb_ref,
    dq_ref,
    near_ref,
    dvert_ref,
    near,
    dvert,
    w_low,
    s_low,
):
    h = pl.program_id(0)
    dim = win_ref.shape[3]
    group = q_ref.shape[1] // dim
    lanes = group * BLOCK
    scaling = 1.0 / math.sqrt(dim)
    near[...] = jnp.zeros_like(near)
    position = lax.broadcasted_iota(jnp.int32, (BLOCK, lanes), 1) % BLOCK
    causal = lax.broadcasted_iota(jnp.int32, (BLOCK, lanes), 0) <= position
    contract_last = (((1,), (1,)), ((), ()))
    contract_first = (((0,), (0,)), ((), ()))
    for j in range(per_device):
        block = first_ref[0] + j

        def stacked(ref):
            return jnp.concatenate(
                [
                    ref[j * BLOCK : (j + 1) * BLOCK, a * dim : (a + 1) * dim]
                    for a in range(group)
                ],
                axis=0,
            )

        q, g, f = stacked(q_ref), stacked(g_ref), stacked(f_ref)
        delta = jnp.sum(
            (g.astype(jnp.float32) * f.astype(jnp.float32)).T, axis=0, keepdims=True
        )
        places, biases = [WDEV * per_device + j], [None]
        for v in range(NV):
            biases.append(jnp.where(vert_ref[h, v] < block, 0.0, NEG))
        for s in range(SLASH_COUNT):
            offset = off_ref[h, s]
            valid = offset > 0
            for v in range(NV):
                valid = valid & (vert_ref[h, v] != block - offset)
            biases.append(jnp.where(valid, 0.0, NEG))
            places.append(WDEV * per_device + j - offset)

        def near_rows(place, kind):
            start = pl.multiple_of((place % per_device) * BLOCK, BLOCK)
            return win_ref[place // per_device, kind, pl.ds(start, BLOCK), :]

        def candidates(kind):
            return jnp.concatenate(
                [near_rows(places[0], kind)]
                + [vb_ref[v, kind] for v in range(NV)]
                + [near_rows(p, kind) for p in places[1:]],
                axis=0,
            )

        keys, values = candidates(0), candidates(1)
        count = len(biases)
        scores = lax.dot_general(keys, q, contract_last, preferred_element_type=jnp.float32)
        masked = []
        for n in range(count):
            part = scores[n * BLOCK : (n + 1) * BLOCK]
            masked.append(
                jnp.where(causal, part, NEG) if n == 0 else part + biases[n]
            )
        top = masked[0]
        for part in masked[1:]:
            top = jnp.maximum(top, part)
        top = jnp.max(top, axis=0, keepdims=True)
        raised = [jnp.exp((part - top) * scaling) for part in masked]
        total = raised[0]
        for part in raised[1:]:
            total = total + part
        inverse = 1.0 / jnp.sum(total, axis=0, keepdims=True)
        weight_grad = lax.dot_general(
            values, g, contract_last, preferred_element_type=jnp.float32
        )
        for n in range(count):
            rows = slice(n * BLOCK, (n + 1) * BLOCK)
            weights = raised[n] * inverse
            w_low[rows, :] = weights.astype(jnp.bfloat16)
            s_low[rows, :] = (weights * (weight_grad[rows] - delta)).astype(jnp.bfloat16)
        score_low = s_low[...]
        dv = jnp.dot(w_low[...], g, preferred_element_type=jnp.float32)
        dk = jnp.dot(score_low, q, preferred_element_type=jnp.float32) * scaling
        dq = lax.dot_general(keys, score_low, contract_first, preferred_element_type=jnp.float32)
        dq = (dq * scaling).T.astype(jnp.bfloat16)
        for a in range(group):
            dq_ref[j * BLOCK : (j + 1) * BLOCK, a * dim : (a + 1) * dim] = dq[
                a * BLOCK : (a + 1) * BLOCK
            ]
        for kind, grads in enumerate((dk, dv)):
            near[places[0], kind] += grads[:BLOCK]
            for s in range(SLASH_COUNT):
                low = (1 + NV + s) * BLOCK
                near[places[1 + s], kind] += grads[low : low + BLOCK]
            for v in range(NV):
                part = grads[(1 + v) * BLOCK : (2 + v) * BLOCK]
                if j == 0:
                    dvert[v, kind] = part
                else:
                    dvert[v, kind] += part
    for p in range((WDEV + 1) * per_device):
        low = (p % per_device) * BLOCK
        near_ref[p // per_device, :, low : low + BLOCK, :] = near[p].astype(jnp.bfloat16)
    dvert_ref[...] = dvert[...].astype(jnp.bfloat16)


def gather_kernel(
    per_device, devices, me_ref, slab_ref, vert_ref, near, back, vb, dk, dv
):
    me = me_ref[0]
    slab = slab_ref[0]
    heads = vert_ref.shape[0]
    dim = vb.shape[3]
    outs = (dk, dv)
    for out in outs:
        out[...] = jnp.zeros_like(out)
    for h in range(heads):
        for v in range(NV):
            block = vert_ref[h, v]
            inner = block % (per_device * devices)

            @pl.when(inner // per_device == me)
            def _():
                region = block // (per_device * devices)
                start = pl.multiple_of((inner % per_device) * BLOCK, BLOCK)
                for kind, out in enumerate(outs):
                    out[region, pl.ds(start, BLOCK), h * dim : (h + 1) * dim] = vb[
                        h * NV + v, kind
                    ]

    here = [
        jnp.where(me + d < devices, 1.0, 0.0).astype(jnp.float32) for d in range(1, WDEV + 1)
    ]
    for kind, out in enumerate(outs):
        current = out[slab].astype(jnp.float32) + near[WDEV, kind].astype(jnp.float32)
        for d in range(1, WDEV + 1):
            current = current + back[d - 1, kind].astype(jnp.float32) * here[d - 1]
        out[slab] = current.astype(jnp.bfloat16)

        @pl.when(me + WDEV >= devices)
        def _():
            prior = out[slab - 1].astype(jnp.float32)
            for d in range(1, WDEV + 1):
                prior = prior + back[d - 1, kind].astype(jnp.float32) * (1.0 - here[d - 1])
            out[slab - 1] = prior.astype(jnp.bfloat16)


def shards(
    queries,
    context_keys,
    context_values,
    forward_output,
    output_cotangent,
    verticals,
    offsets,
    slab_index,
):
    devices = lax.axis_size("ctx")
    me = lax.axis_index("ctx").astype(jnp.int32)
    row_count, columns = queries.shape
    regions, _, features = context_keys.shape
    heads = verticals.shape[0]
    dim = features // heads
    per_device = row_count // BLOCK
    wide = columns // heads
    smem = pl.BlockSpec(memory_space=pltpu.SMEM)
    vmem = pl.BlockSpec(memory_space=pltpu.VMEM)
    hbm = pl.BlockSpec(memory_space=pl.ANY)
    params = pltpu.CompilerParams(vmem_limit_bytes=LIMIT)
    me_arr = me[None]
    low = jnp.bfloat16
    dma = pltpu.SemaphoreType.DMA
    picked, src = pl.pallas_call(
        functools.partial(pick_kernel, per_device, devices),
        out_shape=(
            jax.ShapeDtypeStruct((heads * NV, 2, BLOCK, dim), low),
            jax.ShapeDtypeStruct((2, 2, row_count, features), low),
        ),
        in_specs=[smem, smem, smem, hbm, hbm],
        out_specs=(vmem, vmem),
        scratch_shapes=[dma((heads * NV, 2)), dma((2, 2))],
        compiler_params=params,
        name="pick",
    )(me_arr, slab_index, verticals, context_keys, context_values)
    win, vert = exchange(src, picked.reshape(-1, dim), devices, False)
    first_block = slab_index * (per_device * devices) + me * per_device
    head_rows = pl.BlockSpec((row_count, wide), lambda h, *_: (0, h))
    near_spec = pl.BlockSpec((WDEV + 1, 2, row_count, dim), lambda h, *_: (0, 0, 0, h))
    vert_spec = pl.BlockSpec((NV, 2, BLOCK, dim), lambda h, *_: (h, 0, 0, 0))
    count = 1 + NV + SLASH_COUNT
    lanes = wide // dim * BLOCK
    query_grad, near, vert_grad = pl.pallas_call(
        functools.partial(attend_kernel, per_device),
        out_shape=(
            jax.ShapeDtypeStruct((row_count, columns), low),
            jax.ShapeDtypeStruct((WDEV + 1, 2, row_count, features), low),
            jax.ShapeDtypeStruct((heads * NV, 2, BLOCK, dim), low),
        ),
        grid_spec=pltpu.PrefetchScalarGridSpec(
            num_scalar_prefetch=3,
            grid=(heads,),
            in_specs=[head_rows, head_rows, head_rows, near_spec, vert_spec],
            out_specs=(head_rows, near_spec, vert_spec),
            scratch_shapes=[
                pltpu.VMEM(((WDEV + 1) * per_device, 2, BLOCK, dim), jnp.float32),
                pltpu.VMEM((NV, 2, BLOCK, dim), jnp.float32),
                pltpu.VMEM((count * BLOCK, lanes), low),
                pltpu.VMEM((count * BLOCK, lanes), low),
            ],
        ),
        compiler_params=params,
        name="attend",
    )(
        first_block,
        verticals,
        offsets,
        queries,
        output_cotangent,
        forward_output,
        win,
        vert.reshape(heads * NV, 2, BLOCK, dim),
    )
    back, vert_sum = exchange(near, vert_grad.reshape(-1, dim), devices, True)
    key_grad, value_grad = pl.pallas_call(
        functools.partial(gather_kernel, per_device, devices),
        out_shape=(
            jax.ShapeDtypeStruct((regions, row_count, features), low),
            jax.ShapeDtypeStruct((regions, row_count, features), low),
        ),
        in_specs=[smem, smem, smem, vmem, vmem, vmem],
        out_specs=(vmem, vmem),
        compiler_params=params,
        name="assemble",
    )(
        me_arr,
        slab_index,
        verticals,
        near,
        back,
        vert_sum.reshape(heads * NV, 2, BLOCK, dim),
    )
    return query_grad, key_grad, value_grad


def solution(mesh):
    in_specs = (
        P(("groups", "ctx"), None),
        P("groups", "ctx", None),
        P("groups", "ctx", None),
        P(("groups", "ctx"), None),
        P(("groups", "ctx"), None),
        P("groups", None),
        P("groups", None),
        P("groups"),
    )
    out_specs = (P(("groups", "ctx"), None), P("groups", "ctx", None), P("groups", "ctx", None))
    return jax.shard_map(shards, mesh=mesh, in_specs=in_specs, out_specs=out_specs, check_vma=False)
```

```python
import functools
import math

import jax
import jax.numpy as jnp
from jax import lax
from jax.experimental import pallas as pl
from jax.experimental.pallas import tpu as pltpu
from jax.sharding import PartitionSpec as P

BLOCK = 64
WDEV = 5
NV = 8
SLASH_COUNT = 3
NEG = -1e30
STRIDE = 4
CHUNKS = 4
LIMIT = 48 * 1024 * 1024
MESH = pl.DeviceIdType.MESH


def pick_kernel(per_device, devices, me_ref, slab_ref, vert_ref, ck, cv, pk, src, pick_sem, src_sem):
    me = me_ref[0]
    slab = slab_ref[0]
    heads = vert_ref.shape[0]
    dim = ck.shape[2] // heads
    copies = []
    for which in range(2):
        for kind, ref in enumerate((ck, cv)):
            copy = pltpu.make_async_copy(
                ref.at[slab - which], src.at[which, kind], src_sem.at[which, kind]
            )
            copy.start()
            copies.append(copy)
    pk[...] = jnp.zeros_like(pk)

    def owned_copies(h, v):
        block = vert_ref[h, v]
        region = block // (per_device * devices)
        inner = block % (per_device * devices)
        start = pl.multiple_of((inner % per_device) * BLOCK, BLOCK)
        mine = inner // per_device == me
        made = [
            pltpu.make_async_copy(
                ref.at[region, pl.ds(start, BLOCK), pl.ds(h * dim, dim)],
                pk.at[h * NV + v, kind],
                pick_sem.at[h * NV + v, kind],
            )
            for kind, ref in enumerate((ck, cv))
        ]
        return mine, made

    for h in range(heads):
        for v in range(NV):
            mine, made = owned_copies(h, v)

            @pl.when(mine)
            def _():
                for copy in made:
                    copy.start()

    for copy in copies:
        copy.wait()
    for h in range(heads):
        for v in range(NV):
            mine, made = owned_copies(h, v)

            @pl.when(mine)
            def _():
                for copy in made:
                    copy.wait()


def add_rows(target, target_at, parts, count):
    step = min(count, 64)

    def one(i, carry):
        at = pl.multiple_of(i * step, step)
        total = None
        for ref, start in parts:
            rows = ref[pl.ds(pl.multiple_of(start + at, step), step), :].astype(jnp.float32)
            total = rows if total is None else total + rows
        target[pl.ds(pl.multiple_of(target_at + at, step), step), :] = total.astype(target.dtype)
        return carry

    lax.fori_loop(0, count // step, one, 0)


def exchange_kernel(
    devices,
    back,
    chunks,
    src,
    vert,
    win,
    out,
    got1,
    got2,
    got3,
    sum1,
    sum2,
    joined,
    from_core,
    win_send,
    win_recv,
    own_sem,
    send,
    recv,
    far_send,
    far_recv,
):
    me = lax.axis_index("ctx")
    far = devices // 4
    c, x, z = me % 2, (me // 2) % 2, me // 4
    core_peer = me + 1 - 2 * c
    x_peer = me + 2 - 4 * x
    rows = vert.shape[0] // chunks
    half, quarter, piece = rows // 2, rows // 4, rows // devices

    barrier = pltpu.get_barrier_semaphore()

    def greet(k, carry):
        pl.semaphore_signal(
            barrier, inc=1, device_id={"ctx": (me + k) % devices}, device_id_type=MESH
        )
        return carry

    lax.fori_loop(1, devices, greet, 0)
    pl.semaphore_wait(barrier, devices - 1)

    def remote(a, b, s, r, peer):
        return pltpu.make_async_remote_copy(
            src_ref=a, dst_ref=b, send_sem=s, recv_sem=r, device_id={"ctx": peer}, device_id_type=MESH
        )

    def at(ref, start, count):
        return ref.at[pl.ds(pl.multiple_of(start, count), count)]

    def near(k, a, b, peer):
        return remote(a, b, win_send.at[k], win_recv.at[k], peer)

    def stage(s, k):
        base = k * rows
        own_half = base + c * half
        own_quarter = own_half + x * quarter
        own_piece = own_quarter + z * piece
        if s == 0:
            a, b, peer = at(vert, base + (1 - c) * half, half), at(got1, k * half, half), core_peer
        elif s == 1:
            add_rows(sum1, k * half, [(vert, own_half), (got1, k * half)], half)
            a = at(sum1, k * half + (1 - x) * quarter, quarter)
            b, peer = at(got2, k * quarter, quarter), x_peer
        elif s == 2 or s == 3:
            if s == 2:
                add_rows(
                    sum2, k * quarter, [(sum1, k * half + x * quarter), (got2, k * quarter)], quarter
                )
            else:
                add_rows(
                    out,
                    own_piece,
                    [(sum2, k * quarter + z * piece)]
                    + [(got3, (k * (far - 1) + n) * piece) for n in range(far - 1)],
                    piece,
                )
            made = []
            for n in range(1, far):
                peer_z = (z + n) % far
                if s == 2:
                    a = at(sum2, k * quarter + peer_z * piece, piece)
                    b = at(got3, (k * (far - 1) + n - 1) * piece, piece)
                else:
                    a = b = at(out, own_piece, piece)
                made.append(
                    remote(
                        a,
                        b,
                        far_send.at[s - 2, k, n - 1],
                        far_recv.at[s - 2, k, n - 1],
                        peer_z * 4 + me % 4,
                    )
                )
            return made
        elif s == 4:
            a = b = at(out, own_quarter, quarter)
            peer = x_peer
        else:
            a = b = at(out, own_half, half)
            peer = core_peer
        slot = s if s < 2 else s - 2
        return [remote(a, b, send.at[slot, k], recv.at[slot, k], peer)]

    flying = {}
    for k in range(chunks):
        flying[k] = stage(0, k)
        for copy in flying[k]:
            copy.start()
    pending = []
    own = []
    if back:
        swaps = [
            near(n, src.at[place], from_core.at[n], core_peer)
            for n, place in enumerate((4 - 2 * c, 2 - 2 * c))
        ]
        for copy in swaps:
            copy.start()
        extra = near(
            2, src.at[4 * c], win.at[2], (me + devices - 5 + 4 * c) % devices
        )
        extra.start()
        pending.append(extra)
        for n, d in enumerate((2, 4)):
            swaps[n].wait()

            def join(i, carry):
                at_row = pl.ds(pl.multiple_of(i * 16, 16), 16)
                for kind in range(2):
                    joined[n, kind, at_row, :] = (
                        src[WDEV - d, kind, at_row, :].astype(jnp.float32)
                        + from_core[n, kind, at_row, :].astype(jnp.float32)
                    ).astype(jnp.bfloat16)
                return carry

            lax.fori_loop(0, src.shape[2] // 16, join, 0)
            copy = near(3 + n, joined.at[n], win.at[n], (me + devices - d) % devices)
            copy.start()
            pending.append(copy)
    else:
        own.append(pltpu.make_async_copy(src.at[0], win.at[WDEV], own_sem.at[0]))
        own[0].start()
        for n, d in enumerate((2, 4)):
            copy = near(n, src.at[(me + d) // devices], win.at[WDEV - d], (me + d) % devices)
            copy.start()
            pending.append(copy)
        reach = 1 + 4 * c
        extra = near(
            2, src.at[(me + reach) // devices], win.at[4 - 4 * c], (me + reach) % devices
        )
        extra.start()
    steps = [(s, k) for s in range(1, 7) for k in range(chunks)]
    for s, k in sorted(steps, key=lambda step: (STRIDE * step[0] + step[1], -step[0])):
        for copy in flying[k]:
            copy.wait()
        if s < 6:
            flying[k] = stage(s, k)
            for copy in flying[k]:
                copy.start()
    for copy in own:
        copy.wait()
    if back:
        for copy in pending:
            copy.wait()
    else:
        swaps = []
        for n, d in enumerate((2, 4)):
            pending[n].wait()
            place = 2 + 2 * c if n == 0 else 2 * c
            copy = near(3 + n, win.at[WDEV - d], win.at[place], core_peer)
            copy.start()
            swaps.append(copy)
        extra.wait()
        for copy in swaps:
            copy.wait()


def exchange(src, vert, devices, back):
    rows, dim = vert.shape
    far = devices // 4
    chunks = max(1, min(CHUNKS, rows // (devices * 16)))
    piece = rows // chunks // devices
    slots = 3 if back else WDEV + 1
    slot = (2,) + src.shape[1:] if back else (1, 1, 16, src.shape[3])
    dma = pltpu.SemaphoreType.DMA
    vmem = pl.BlockSpec(memory_space=pltpu.VMEM)
    low = jnp.bfloat16
    return pl.pallas_call(
        functools.partial(exchange_kernel, devices, back, chunks),
        out_shape=(
            jax.ShapeDtypeStruct((slots,) + src.shape[1:], low),
            jax.ShapeDtypeStruct((rows, dim), low),
        ),
        in_specs=[vmem, vmem],
        out_specs=(vmem, vmem),
        scratch_shapes=[
            pltpu.VMEM((rows // 2, dim), low),
            pltpu.VMEM((rows // 4, dim), low),
            pltpu.VMEM((chunks * (far - 1) * piece, dim), low),
            pltpu.VMEM((rows // 2, dim), low),
            pltpu.VMEM((rows // 4, dim), low),
            pltpu.VMEM(slot, low),
            pltpu.VMEM(slot, low),
            dma((5,)),
            dma((5,)),
            dma((1,)),
            dma((4, chunks)),
            dma((4, chunks)),
            dma((2, chunks, far - 1)),
            dma((2, chunks, far - 1)),
        ],
        compiler_params=pltpu.CompilerParams(
            collective_id=1 if back else 0, has_side_effects=True, vmem_limit_bytes=LIMIT
        ),
        name="send_back" if back else "send_out",
    )(src, vert)


def attend_kernel(
    per_device,
    first_ref,
    vert_ref,
    off_ref,
    q_ref,
    g_ref,
    f_ref,
    win_ref,
    vb_ref,
    dq_ref,
    near_ref,
    dvert_ref,
    near,
    dvert,
    w_low,
    s_low,
):
    h = pl.program_id(0)
    dim = win_ref.shape[3]
    group = q_ref.shape[1] // dim
    lanes = group * BLOCK
    scaling = 1.0 / math.sqrt(dim)
    near[...] = jnp.zeros_like(near)
    position = lax.broadcasted_iota(jnp.int32, (BLOCK, lanes), 1) % BLOCK
    causal = lax.broadcasted_iota(jnp.int32, (BLOCK, lanes), 0) <= position
    contract_last = (((1,), (1,)), ((), ()))
    contract_first = (((0,), (0,)), ((), ()))
    for j in range(per_device):
        block = first_ref[0] + j

        def stacked(ref):
            return jnp.concatenate(
                [
                    ref[j * BLOCK : (j + 1) * BLOCK, a * dim : (a + 1) * dim]
                    for a in range(group)
                ],
                axis=0,
            )

        q, g, f = stacked(q_ref), stacked(g_ref), stacked(f_ref)
        delta = jnp.sum(
            (g.astype(jnp.float32) * f.astype(jnp.float32)).T, axis=0, keepdims=True
        )
        places, biases = [WDEV * per_device + j], [None]
        for v in range(NV):
            biases.append(jnp.where(vert_ref[h, v] < block, 0.0, NEG))
        for s in range(SLASH_COUNT):
            offset = off_ref[h, s]
            valid = offset > 0
            for v in range(NV):
                valid = valid & (vert_ref[h, v] != block - offset)
            biases.append(jnp.where(valid, 0.0, NEG))
            places.append(WDEV * per_device + j - offset)

        def near_rows(place, kind):
            start = pl.multiple_of((place % per_device) * BLOCK, BLOCK)
            return win_ref[place // per_device, kind, pl.ds(start, BLOCK), :]

        def candidates(kind):
            return jnp.concatenate(
                [near_rows(places[0], kind)]
                + [vb_ref[v, kind] for v in range(NV)]
                + [near_rows(p, kind) for p in places[1:]],
                axis=0,
            )

        keys, values = candidates(0), candidates(1)
        count = len(biases)
        scores = lax.dot_general(keys, q, contract_last, preferred_element_type=jnp.float32)
        masked = []
        for n in range(count):
            part = scores[n * BLOCK : (n + 1) * BLOCK]
            masked.append(
                jnp.where(causal, part, NEG) if n == 0 else part + biases[n]
            )
        top = masked[0]
        for part in masked[1:]:
            top = jnp.maximum(top, part)
        top = jnp.max(top, axis=0, keepdims=True)
        raised = [jnp.exp((part - top) * scaling) for part in masked]
        total = raised[0]
        for part in raised[1:]:
            total = total + part
        inverse = 1.0 / jnp.sum(total, axis=0, keepdims=True)
        weight_grad = lax.dot_general(
            values, g, contract_last, preferred_element_type=jnp.float32
        )
        for n in range(count):
            rows = slice(n * BLOCK, (n + 1) * BLOCK)
            weights = raised[n] * inverse
            w_low[rows, :] = weights.astype(jnp.bfloat16)
            s_low[rows, :] = (weights * (weight_grad[rows] - delta)).astype(jnp.bfloat16)
        score_low = s_low[...]
        dv = jnp.dot(w_low[...], g, preferred_element_type=jnp.float32)
        dk = jnp.dot(score_low, q, preferred_element_type=jnp.float32) * scaling
        dq = lax.dot_general(keys, score_low, contract_first, preferred_element_type=jnp.float32)
        dq = (dq * scaling).T.astype(jnp.bfloat16)
        for a in range(group):
            dq_ref[j * BLOCK : (j + 1) * BLOCK, a * dim : (a + 1) * dim] = dq[
                a * BLOCK : (a + 1) * BLOCK
            ]
        for kind, grads in enumerate((dk, dv)):
            near[places[0], kind] += grads[:BLOCK]
            for s in range(SLASH_COUNT):
                low = (1 + NV + s) * BLOCK
                near[places[1 + s], kind] += grads[low : low + BLOCK]
            for v in range(NV):
                part = grads[(1 + v) * BLOCK : (2 + v) * BLOCK]
                if j == 0:
                    dvert[v, kind] = part
                else:
                    dvert[v, kind] += part
    for p in range((WDEV + 1) * per_device):
        low = (p % per_device) * BLOCK
        near_ref[p // per_device, :, low : low + BLOCK, :] = near[p].astype(jnp.bfloat16)
    dvert_ref[...] = dvert[...].astype(jnp.bfloat16)


def gather_kernel(
    per_device, devices, me_ref, slab_ref, vert_ref, near, back, vb, dk, dv
):
    me = me_ref[0]
    slab = slab_ref[0]
    heads = vert_ref.shape[0]
    dim = vb.shape[3]
    outs = (dk, dv)
    for out in outs:
        out[...] = jnp.zeros_like(out)
    for h in range(heads):
        for v in range(NV):
            block = vert_ref[h, v]
            inner = block % (per_device * devices)

            @pl.when(inner // per_device == me)
            def _():
                region = block // (per_device * devices)
                start = pl.multiple_of((inner % per_device) * BLOCK, BLOCK)
                for kind, out in enumerate(outs):
                    out[region, pl.ds(start, BLOCK), h * dim : (h + 1) * dim] = vb[
                        h * NV + v, kind
                    ]

    wrapped = [
        jnp.where(me + reach >= devices, 1.0, 0.0).astype(jnp.float32)
        for reach in (2, 4, 1 + 4 * (me % 2))
    ]
    for kind, out in enumerate(outs):
        current = out[slab].astype(jnp.float32) + near[WDEV, kind].astype(jnp.float32)
        for n in range(3):
            current = current + back[n, kind].astype(jnp.float32) * (1.0 - wrapped[n])
        out[slab] = current.astype(jnp.bfloat16)

        @pl.when(me + WDEV >= devices)
        def _():
            prior = out[slab - 1].astype(jnp.float32)
            for n in range(3):
                prior = prior + back[n, kind].astype(jnp.float32) * wrapped[n]
            out[slab - 1] = prior.astype(jnp.bfloat16)


def shards(
    queries,
    context_keys,
    context_values,
    forward_output,
    output_cotangent,
    verticals,
    offsets,
    slab_index,
):
    devices = lax.axis_size("ctx")
    me = lax.axis_index("ctx").astype(jnp.int32)
    row_count, columns = queries.shape
    regions, _, features = context_keys.shape
    heads = verticals.shape[0]
    dim = features // heads
    per_device = row_count // BLOCK
    wide = columns // heads
    smem = pl.BlockSpec(memory_space=pltpu.SMEM)
    vmem = pl.BlockSpec(memory_space=pltpu.VMEM)
    hbm = pl.BlockSpec(memory_space=pltpu.HBM)
    params = pltpu.CompilerParams(vmem_limit_bytes=LIMIT)
    me_arr = me[None]
    low = jnp.bfloat16
    dma = pltpu.SemaphoreType.DMA
    picked, src = pl.pallas_call(
        functools.partial(pick_kernel, per_device, devices),
        out_shape=(
            jax.ShapeDtypeStruct((heads * NV, 2, BLOCK, dim), low),
            jax.ShapeDtypeStruct((2, 2, row_count, features), low),
        ),
        in_specs=[smem, smem, smem, hbm, hbm],
        out_specs=(vmem, vmem),
        scratch_shapes=[dma((heads * NV, 2)), dma((2, 2))],
        compiler_params=params,
        name="pick",
    )(me_arr, slab_index, verticals, context_keys, context_values)
    win, vert = exchange(src, picked.reshape(-1, dim), devices, False)
    first_block = slab_index * (per_device * devices) + me * per_device
    head_rows = pl.BlockSpec((row_count, wide), lambda h, *_: (0, h))
    near_spec = pl.BlockSpec((WDEV + 1, 2, row_count, dim), lambda h, *_: (0, 0, 0, h))
    vert_spec = pl.BlockSpec((NV, 2, BLOCK, dim), lambda h, *_: (h, 0, 0, 0))
    count = 1 + NV + SLASH_COUNT
    lanes = wide // dim * BLOCK
    query_grad, near, vert_grad = pl.pallas_call(
        functools.partial(attend_kernel, per_device),
        out_shape=(
            jax.ShapeDtypeStruct((row_count, columns), low),
            jax.ShapeDtypeStruct((WDEV + 1, 2, row_count, features), low),
            jax.ShapeDtypeStruct((heads * NV, 2, BLOCK, dim), low),
        ),
        grid_spec=pltpu.PrefetchScalarGridSpec(
            num_scalar_prefetch=3,
            grid=(heads,),
            in_specs=[head_rows, head_rows, head_rows, near_spec, vert_spec],
            out_specs=(head_rows, near_spec, vert_spec),
            scratch_shapes=[
                pltpu.VMEM(((WDEV + 1) * per_device, 2, BLOCK, dim), jnp.float32),
                pltpu.VMEM((NV, 2, BLOCK, dim), jnp.float32),
                pltpu.VMEM((count * BLOCK, lanes), low),
                pltpu.VMEM((count * BLOCK, lanes), low),
            ],
        ),
        compiler_params=params,
        name="attend",
    )(
        first_block,
        verticals,
        offsets,
        queries,
        output_cotangent,
        forward_output,
        win,
        vert.reshape(heads * NV, 2, BLOCK, dim),
    )
    back, vert_sum = exchange(near, vert_grad.reshape(-1, dim), devices, True)
    key_grad, value_grad = pl.pallas_call(
        functools.partial(gather_kernel, per_device, devices),
        out_shape=(
            jax.ShapeDtypeStruct((regions, row_count, features), low),
            jax.ShapeDtypeStruct((regions, row_count, features), low),
        ),
        in_specs=[smem, smem, smem, vmem, vmem, vmem],
        out_specs=(vmem, vmem),
        compiler_params=params,
        name="assemble",
    )(
        me_arr,
        slab_index,
        verticals,
        near,
        back,
        vert_sum.reshape(heads * NV, 2, BLOCK, dim),
    )
    return query_grad, key_grad, value_grad


def solution(mesh):
    in_specs = (
        P(("groups", "ctx"), None),
        P("groups", "ctx", None),
        P("groups", "ctx", None),
        P(("groups", "ctx"), None),
        P(("groups", "ctx"), None),
        P("groups", None),
        P("groups", None),
        P("groups"),
    )
    out_specs = (P(("groups", "ctx"), None), P("groups", "ctx", None), P("groups", "ctx", None))
    return jax.shard_map(shards, mesh=mesh, in_specs=in_specs, out_specs=out_specs, check_vma=False)
```

```python
import functools
import math

import jax
import jax.numpy as jnp
from jax import lax
from jax.experimental import pallas as pl
from jax.experimental.pallas import tpu as pltpu
from jax.sharding import PartitionSpec as P

BLOCK = 64
WDEV = 5
NV = 8
SLASH_COUNT = 3
NEG = -1e30
CHUNKS = 4
LIMIT = 48 * 1024 * 1024
MESH = pl.DeviceIdType.MESH


def pick_kernel(per_device, devices, me_ref, slab_ref, vert_ref, ck, cv, pk, src, pick_sem, src_sem):
    me = me_ref[0]
    slab = slab_ref[0]
    heads = vert_ref.shape[0]
    dim = ck.shape[2] // heads
    copies = []
    for which in range(2):
        for kind, ref in enumerate((ck, cv)):
            copy = pltpu.make_async_copy(
                ref.at[slab - which], src.at[which, kind], src_sem.at[which, kind]
            )
            copy.start()
            copies.append(copy)
    pk[...] = jnp.zeros_like(pk)

    def owned_copies(h, v):
        block = vert_ref[h, v]
        region = block // (per_device * devices)
        inner = block % (per_device * devices)
        start = pl.multiple_of((inner % per_device) * BLOCK, BLOCK)
        mine = inner // per_device == me
        made = [
            pltpu.make_async_copy(
                ref.at[region, pl.ds(start, BLOCK), pl.ds(h * dim, dim)],
                pk.at[h * NV + v, kind],
                pick_sem.at[h * NV + v, kind],
            )
            for kind, ref in enumerate((ck, cv))
        ]
        return mine, made

    for h in range(heads):
        for v in range(NV):
            mine, made = owned_copies(h, v)

            @pl.when(mine)
            def _():
                for copy in made:
                    copy.start()

    for copy in copies:
        copy.wait()
    for h in range(heads):
        for v in range(NV):
            mine, made = owned_copies(h, v)

            @pl.when(mine)
            def _():
                for copy in made:
                    copy.wait()


def add_rows(target, target_at, parts, count):
    step = min(count, 64)

    def one(i, carry):
        at = pl.multiple_of(i * step, step)
        total = None
        for ref, start in parts:
            rows = ref[pl.ds(pl.multiple_of(start + at, step), step), :].astype(jnp.float32)
            total = rows if total is None else total + rows
        target[pl.ds(pl.multiple_of(target_at + at, step), step), :] = total.astype(target.dtype)
        return carry

    lax.fori_loop(0, count // step, one, 0)


def exchange_kernel(
    devices,
    back,
    chunks,
    src,
    vert,
    win,
    out,
    got1,
    got2,
    got3,
    sum1,
    sum2,
    joined,
    from_core,
    win_send,
    win_recv,
    own_sem,
    send,
    recv,
    far_send,
    far_recv,
):
    me = lax.axis_index("ctx")
    far = devices // 4
    c, x, z = me % 2, (me // 2) % 2, me // 4
    core_peer = me + 1 - 2 * c
    x_peer = me + 2 - 4 * x
    rows = vert.shape[0] // chunks
    half, quarter, piece = rows // 2, rows // 4, rows // devices

    barrier = pltpu.get_barrier_semaphore()

    def greet(k, carry):
        pl.semaphore_signal(
            barrier, inc=1, device_id={"ctx": (me + k) % devices}, device_id_type=MESH
        )
        return carry

    lax.fori_loop(1, devices, greet, 0)
    pl.semaphore_wait(barrier, devices - 1)

    def remote(a, b, s, r, peer):
        return pltpu.make_async_remote_copy(
            src_ref=a, dst_ref=b, send_sem=s, recv_sem=r, device_id={"ctx": peer}, device_id_type=MESH
        )

    def at(ref, start, count):
        return ref.at[pl.ds(pl.multiple_of(start, count), count)]

    def near(k, a, b, peer):
        return remote(a, b, win_send.at[k], win_recv.at[k], peer)

    def stage(s, k):
        base = k * rows
        own_half = base + c * half
        own_quarter = own_half + x * quarter
        own_piece = own_quarter + z * piece
        if s == 0:
            a, b, peer = at(vert, base + (1 - c) * half, half), at(got1, k * half, half), core_peer
        elif s == 1:
            add_rows(sum1, k * half, [(vert, own_half), (got1, k * half)], half)
            a = at(sum1, k * half + (1 - x) * quarter, quarter)
            b, peer = at(got2, k * quarter, quarter), x_peer
        elif s == 2 or s == 3:
            if s == 2:
                add_rows(
                    sum2, k * quarter, [(sum1, k * half + x * quarter), (got2, k * quarter)], quarter
                )
            else:
                add_rows(
                    out,
                    own_piece,
                    [(sum2, k * quarter + z * piece)]
                    + [(got3, (k * (far - 1) + n) * piece) for n in range(far - 1)],
                    piece,
                )
            made = []
            for n in range(1, far):
                peer_z = (z + n) % far
                if s == 2:
                    a = at(sum2, k * quarter + peer_z * piece, piece)
                    b = at(got3, (k * (far - 1) + n - 1) * piece, piece)
                else:
                    a = b = at(out, own_piece, piece)
                made.append(
                    remote(
                        a,
                        b,
                        far_send.at[s - 2, k, n - 1],
                        far_recv.at[s - 2, k, n - 1],
                        peer_z * 4 + me % 4,
                    )
                )
            return made
        elif s == 4:
            a = b = at(out, own_quarter, quarter)
            peer = x_peer
        else:
            a = b = at(out, own_half, half)
            peer = core_peer
        slot = s if s < 2 else s - 2
        return [remote(a, b, send.at[slot, k], recv.at[slot, k], peer)]

    flying = {}
    for k in range(chunks):
        flying[k] = stage(0, k)
        for copy in flying[k]:
            copy.start()
    def joined_rows(n, parts):
        def join(i, carry):
            at_row = pl.ds(pl.multiple_of(i * 16, 16), 16)
            for kind in range(2):
                total = None
                for ref, place, weight in parts:
                    term = ref[place, kind, at_row, :].astype(jnp.float32)
                    term = term if weight is None else term * weight
                    total = term if total is None else total + term
                joined[n, kind, at_row, :] = total.astype(jnp.bfloat16)
            return carry

        lax.fori_loop(0, src.shape[2] // 16, join, 0)

    if back:
        swaps = [
            near(n, src.at[place], from_core.at[n], core_peer)
            for n, place in enumerate((4 - 2 * c, 2 - 2 * c))
        ]
        for copy in swaps:
            copy.start()
        extra = near(2, src.at[4 * c], win.at[2], (me + devices - 5 + 4 * c) % devices)
        extra.start()
        across = near(3, joined.at[0], win.at[0], x_peer)
        along = near(4, joined.at[1], win.at[1], (me + devices - 4) % devices)
        swaps[0].wait()
        joined_rows(0, [(src, WDEV - 2, None), (from_core, 0, None)])
        swaps[1].wait()
    else:
        own = pltpu.make_async_copy(src.at[0], win.at[WDEV], own_sem.at[0])
        own.start()
        along = near(0, src.at[(me + 4) // devices], win.at[WDEV - 4], (me + 4) % devices)
        along.start()
        across = near(1, src.at[0], win.at[WDEV - 2], x_peer)
        passed = near(1, win.at[WDEV - 4], win.at[WDEV - 2], x_peer)
        reach = 1 + 4 * c
        extra = near(2, src.at[(me + reach) // devices], win.at[4 - 4 * c], (me + reach) % devices)
        handed = near(2, win.at[WDEV - 4], win.at[0], (me + 1) % devices)
        late = c * (1 - x)

        @pl.when(x == 0)
        def _():
            across.start()

        @pl.when(late == 0)
        def _():
            extra.start()

        swap_far = near(4, win.at[WDEV - 4], win.at[2 * c], core_peer)
        swap_next = near(3, win.at[WDEV - 2], win.at[2 + 2 * c], core_peer)

    def between(s):
        if back:
            if s == 1:
                across.start()
            elif s == 3:
                across.wait()
                merge = jnp.where(x == 1, 1.0, 0.0).astype(jnp.float32)
                joined_rows(1, [(src, WDEV - 4, None), (from_core, 1, None), (win, 0, merge)])
                along.start()
            elif s == 6:
                along.wait()
                extra.wait()
        elif s == 2:
            along.wait()
            swap_far.start()

            @pl.when(x == 1)
            def _():
                passed.start()

            @pl.when(late == 1)
            def _():
                handed.start()
        elif s == 4:
            across.wait()
            swap_next.start()
        elif s == 6:
            extra.wait()
            swap_far.wait()
            swap_next.wait()
            own.wait()

    for s in range(1, 7):
        for k in range(chunks):
            for copy in flying[k]:
                copy.wait()
            if s < 6:
                flying[k] = stage(s, k)
                for copy in flying[k]:
                    copy.start()
        between(s)


def exchange(src, vert, devices, back):
    rows, dim = vert.shape
    far = devices // 4
    chunks = max(1, min(CHUNKS, rows // (devices * 16)))
    piece = rows // chunks // devices
    slots = 3 if back else WDEV + 1
    slot = (2,) + src.shape[1:] if back else (1, 1, 16, src.shape[3])
    dma = pltpu.SemaphoreType.DMA
    vmem = pl.BlockSpec(memory_space=pltpu.VMEM)
    low = jnp.bfloat16
    return pl.pallas_call(
        functools.partial(exchange_kernel, devices, back, chunks),
        out_shape=(
            jax.ShapeDtypeStruct((slots,) + src.shape[1:], low),
            jax.ShapeDtypeStruct((rows, dim), low),
        ),
        in_specs=[vmem, vmem],
        out_specs=(vmem, vmem),
        scratch_shapes=[
            pltpu.VMEM((rows // 2, dim), low),
            pltpu.VMEM((rows // 4, dim), low),
            pltpu.VMEM((chunks * (far - 1) * piece, dim), low),
            pltpu.VMEM((rows // 2, dim), low),
            pltpu.VMEM((rows // 4, dim), low),
            pltpu.VMEM(slot, low),
            pltpu.VMEM(slot, low),
            dma((5,)),
            dma((5,)),
            dma((1,)),
            dma((4, chunks)),
            dma((4, chunks)),
            dma((2, chunks, far - 1)),
            dma((2, chunks, far - 1)),
        ],
        compiler_params=pltpu.CompilerParams(
            collective_id=1 if back else 0, has_side_effects=True, vmem_limit_bytes=LIMIT
        ),
        name="send_back" if back else "send_out",
    )(src, vert)


def attend_kernel(
    per_device,
    first_ref,
    vert_ref,
    off_ref,
    q_ref,
    g_ref,
    f_ref,
    win_ref,
    vb_ref,
    dq_ref,
    near_ref,
    dvert_ref,
    near,
    dvert,
    w_low,
    s_low,
):
    h = pl.program_id(0)
    dim = vb_ref.shape[3]
    columns = pl.ds(pl.multiple_of(h * dim, dim), dim)
    group = q_ref.shape[1] // dim
    lanes = group * BLOCK
    scaling = 1.0 / math.sqrt(dim)
    near[...] = jnp.zeros_like(near)
    position = lax.broadcasted_iota(jnp.int32, (BLOCK, lanes), 1) % BLOCK
    causal = lax.broadcasted_iota(jnp.int32, (BLOCK, lanes), 0) <= position
    contract_last = (((1,), (1,)), ((), ()))
    contract_first = (((0,), (0,)), ((), ()))
    for j in range(per_device):
        block = first_ref[0] + j

        def stacked(ref):
            return jnp.concatenate(
                [
                    ref[j * BLOCK : (j + 1) * BLOCK, a * dim : (a + 1) * dim]
                    for a in range(group)
                ],
                axis=0,
            )

        q, g, f = stacked(q_ref), stacked(g_ref), stacked(f_ref)
        delta = jnp.sum(
            (g.astype(jnp.float32) * f.astype(jnp.float32)).T, axis=0, keepdims=True
        )
        places, biases = [WDEV * per_device + j], [None]
        for v in range(NV):
            biases.append(jnp.where(vert_ref[h, v] < block, 0.0, NEG))
        for s in range(SLASH_COUNT):
            offset = off_ref[h, s]
            valid = offset > 0
            for v in range(NV):
                valid = valid & (vert_ref[h, v] != block - offset)
            biases.append(jnp.where(valid, 0.0, NEG))
            places.append(WDEV * per_device + j - offset)

        def near_rows(place, kind):
            start = pl.multiple_of((place % per_device) * BLOCK, BLOCK)
            return win_ref[place // per_device, kind, pl.ds(start, BLOCK), columns]

        def candidates(kind):
            return jnp.concatenate(
                [near_rows(places[0], kind)]
                + [vb_ref[v, kind] for v in range(NV)]
                + [near_rows(p, kind) for p in places[1:]],
                axis=0,
            )

        keys, values = candidates(0), candidates(1)
        count = len(biases)
        scores = lax.dot_general(keys, q, contract_last, preferred_element_type=jnp.float32)
        masked = []
        for n in range(count):
            part = scores[n * BLOCK : (n + 1) * BLOCK]
            masked.append(
                jnp.where(causal, part, NEG) if n == 0 else part + biases[n]
            )
        top = masked[0]
        for part in masked[1:]:
            top = jnp.maximum(top, part)
        top = jnp.max(top, axis=0, keepdims=True)
        raised = [jnp.exp((part - top) * scaling) for part in masked]
        total = raised[0]
        for part in raised[1:]:
            total = total + part
        inverse = 1.0 / jnp.sum(total, axis=0, keepdims=True)
        weight_grad = lax.dot_general(
            values, g, contract_last, preferred_element_type=jnp.float32
        )
        for n in range(count):
            rows = slice(n * BLOCK, (n + 1) * BLOCK)
            weights = raised[n] * inverse
            w_low[rows, :] = weights.astype(jnp.bfloat16)
            s_low[rows, :] = (weights * (weight_grad[rows] - delta)).astype(jnp.bfloat16)
        score_low = s_low[...]
        dv = jnp.dot(w_low[...], g, preferred_element_type=jnp.float32)
        dk = jnp.dot(score_low, q, preferred_element_type=jnp.float32) * scaling
        dq = lax.dot_general(keys, score_low, contract_first, preferred_element_type=jnp.float32)
        dq = (dq * scaling).T.astype(jnp.bfloat16)
        for a in range(group):
            dq_ref[j * BLOCK : (j + 1) * BLOCK, a * dim : (a + 1) * dim] = dq[
                a * BLOCK : (a + 1) * BLOCK
            ]
        for kind, grads in enumerate((dk, dv)):
            near[places[0], kind] += grads[:BLOCK]
            for s in range(SLASH_COUNT):
                low = (1 + NV + s) * BLOCK
                near[places[1 + s], kind] += grads[low : low + BLOCK]
            for v in range(NV):
                part = grads[(1 + v) * BLOCK : (2 + v) * BLOCK]
                if j == 0:
                    dvert[v, kind] = part
                else:
                    dvert[v, kind] += part
    for p in range((WDEV + 1) * per_device):
        low = (p % per_device) * BLOCK
        near_ref[p // per_device, :, low : low + BLOCK, columns] = near[p].astype(jnp.bfloat16)
    dvert_ref[...] = dvert[...].astype(jnp.bfloat16)


def gather_kernel(
    per_device, devices, me_ref, slab_ref, vert_ref, near, back, vb, dk, dv
):
    me = me_ref[0]
    slab = slab_ref[0]
    heads = vert_ref.shape[0]
    dim = vb.shape[3]
    outs = (dk, dv)
    for out in outs:
        out[...] = jnp.zeros_like(out)
    for h in range(heads):
        for v in range(NV):
            block = vert_ref[h, v]
            inner = block % (per_device * devices)

            @pl.when(inner // per_device == me)
            def _():
                region = block // (per_device * devices)
                start = pl.multiple_of((inner % per_device) * BLOCK, BLOCK)
                for kind, out in enumerate(outs):
                    out[region, pl.ds(start, BLOCK), h * dim : (h + 1) * dim] = vb[
                        h * NV + v, kind
                    ]

    def flag(yes):
        return jnp.where(yes, 1.0, 0.0).astype(jnp.float32)

    far_wraps = me + 4 >= devices
    extra_wraps = me + 1 + 4 * (me % 2) >= devices
    here = [flag((me // 2) % 2 == 0), flag(jnp.logical_not(far_wraps)), flag(jnp.logical_not(extra_wraps))]
    wrapped = [None, flag(far_wraps), flag(extra_wraps)]
    for kind, out in enumerate(outs):
        current = out[slab].astype(jnp.float32) + near[WDEV, kind].astype(jnp.float32)
        for n in range(3):
            current = current + back[n, kind].astype(jnp.float32) * here[n]
        out[slab] = current.astype(jnp.bfloat16)

        @pl.when(me + WDEV >= devices)
        def _():
            prior = out[slab - 1].astype(jnp.float32)
            for n in range(1, 3):
                prior = prior + back[n, kind].astype(jnp.float32) * wrapped[n]
            out[slab - 1] = prior.astype(jnp.bfloat16)


def shards(
    queries,
    context_keys,
    context_values,
    forward_output,
    output_cotangent,
    verticals,
    offsets,
    slab_index,
):
    devices = lax.axis_size("ctx")
    me = lax.axis_index("ctx").astype(jnp.int32)
    row_count, columns = queries.shape
    regions, _, features = context_keys.shape
    heads = verticals.shape[0]
    dim = features // heads
    per_device = row_count // BLOCK
    wide = columns // heads
    smem = pl.BlockSpec(memory_space=pltpu.SMEM)
    vmem = pl.BlockSpec(memory_space=pltpu.VMEM)
    hbm = pl.BlockSpec(memory_space=pltpu.HBM)
    params = pltpu.CompilerParams(vmem_limit_bytes=LIMIT)
    me_arr = me[None]
    low = jnp.bfloat16
    dma = pltpu.SemaphoreType.DMA
    picked, src = pl.pallas_call(
        functools.partial(pick_kernel, per_device, devices),
        out_shape=(
            jax.ShapeDtypeStruct((heads * NV, 2, BLOCK, dim), low),
            jax.ShapeDtypeStruct((2, 2, row_count, features), low),
        ),
        in_specs=[smem, smem, smem, hbm, hbm],
        out_specs=(vmem, vmem),
        scratch_shapes=[dma((heads * NV, 2)), dma((2, 2))],
        compiler_params=pltpu.CompilerParams(vmem_limit_bytes=52 * 1024 * 1024),
        name="pick",
    )(me_arr, slab_index, verticals, context_keys, context_values)
    win, vert = exchange(src, picked.reshape(-1, dim), devices, False)
    first_block = slab_index * (per_device * devices) + me * per_device
    head_rows = pl.BlockSpec((row_count, wide), lambda h, *_: (0, h))
    vert_spec = pl.BlockSpec((NV, 2, BLOCK, dim), lambda h, *_: (h, 0, 0, 0))
    count = 1 + NV + SLASH_COUNT
    lanes = wide // dim * BLOCK
    query_grad, near, vert_grad = pl.pallas_call(
        functools.partial(attend_kernel, per_device),
        out_shape=(
            jax.ShapeDtypeStruct((row_count, columns), low),
            jax.ShapeDtypeStruct((WDEV + 1, 2, row_count, features), low),
            jax.ShapeDtypeStruct((heads * NV, 2, BLOCK, dim), low),
        ),
        grid_spec=pltpu.PrefetchScalarGridSpec(
            num_scalar_prefetch=3,
            grid=(heads,),
            in_specs=[head_rows, head_rows, head_rows, vmem, vert_spec],
            out_specs=(head_rows, vmem, vert_spec),
            scratch_shapes=[
                pltpu.VMEM(((WDEV + 1) * per_device, 2, BLOCK, dim), jnp.float32),
                pltpu.VMEM((NV, 2, BLOCK, dim), jnp.float32),
                pltpu.VMEM((count * BLOCK, lanes), low),
                pltpu.VMEM((count * BLOCK, lanes), low),
            ],
        ),
        compiler_params=pltpu.CompilerParams(vmem_limit_bytes=32 * 1024 * 1024),
        name="attend",
    )(
        first_block,
        verticals,
        offsets,
        queries,
        output_cotangent,
        forward_output,
        win,
        vert.reshape(heads * NV, 2, BLOCK, dim),
    )
    back, vert_sum = exchange(near, vert_grad.reshape(-1, dim), devices, True)
    key_grad, value_grad = pl.pallas_call(
        functools.partial(gather_kernel, per_device, devices),
        out_shape=(
            jax.ShapeDtypeStruct((regions, row_count, features), low),
            jax.ShapeDtypeStruct((regions, row_count, features), low),
        ),
        in_specs=[smem, smem, smem, vmem, vmem, vmem],
        out_specs=(vmem, vmem),
        compiler_params=params,
        name="assemble",
    )(
        me_arr,
        slab_index,
        verticals,
        near,
        back,
        vert_sum.reshape(heads * NV, 2, BLOCK, dim),
    )
    return query_grad, key_grad, value_grad


def solution(mesh):
    in_specs = (
        P(("groups", "ctx"), None),
        P("groups", "ctx", None),
        P("groups", "ctx", None),
        P(("groups", "ctx"), None),
        P(("groups", "ctx"), None),
        P("groups", None),
        P("groups", None),
        P("groups"),
    )
    out_specs = (P(("groups", "ctx"), None), P("groups", "ctx", None), P("groups", "ctx", None))
    return jax.shard_map(shards, mesh=mesh, in_specs=in_specs, out_specs=out_specs, check_vma=False)
```

```python
import functools
import math

import jax
import jax.numpy as jnp
from jax import lax
from jax.experimental import pallas as pl
from jax.experimental.pallas import tpu as pltpu
from jax.sharding import PartitionSpec as P

BLOCK = 64
WDEV = 5
NV = 8
SLASH_COUNT = 3
NEG = -1e30
CHUNKS = 4
LIMIT = 48 * 1024 * 1024
MESH = pl.DeviceIdType.MESH


def pick_kernel(per_device, devices, me_ref, slab_ref, vert_ref, ck, cv, pk, src, pick_sem, src_sem):
    me = me_ref[0]
    slab = slab_ref[0]
    heads = vert_ref.shape[0]
    dim = ck.shape[2] // heads
    copies = []
    for which in range(2):
        for kind, ref in enumerate((ck, cv)):
            copy = pltpu.make_async_copy(
                ref.at[slab - which], src.at[which, kind], src_sem.at[which, kind]
            )
            copy.start()
            copies.append(copy)
    pk[...] = jnp.zeros_like(pk)

    def owned_copies(h, v):
        block = vert_ref[h, v]
        region = block // (per_device * devices)
        inner = block % (per_device * devices)
        start = pl.multiple_of((inner % per_device) * BLOCK, BLOCK)
        mine = inner // per_device == me
        made = [
            pltpu.make_async_copy(
                ref.at[region, pl.ds(start, BLOCK), pl.ds(h * dim, dim)],
                pk.at[h * NV + v, kind],
                pick_sem.at[h * NV + v, kind],
            )
            for kind, ref in enumerate((ck, cv))
        ]
        return mine, made

    for h in range(heads):
        for v in range(NV):
            mine, made = owned_copies(h, v)

            @pl.when(mine)
            def _():
                for copy in made:
                    copy.start()

    for copy in copies:
        copy.wait()
    for h in range(heads):
        for v in range(NV):
            mine, made = owned_copies(h, v)

            @pl.when(mine)
            def _():
                for copy in made:
                    copy.wait()


def add_rows(target, target_at, parts, count):
    step = min(count, 64)

    def one(i, carry):
        at = pl.multiple_of(i * step, step)
        total = None
        for ref, start in parts:
            rows = ref[pl.ds(pl.multiple_of(start + at, step), step), :].astype(jnp.float32)
            total = rows if total is None else total + rows
        target[pl.ds(pl.multiple_of(target_at + at, step), step), :] = total.astype(target.dtype)
        return carry

    lax.fori_loop(0, count // step, one, 0)


def exchange_kernel(
    devices,
    back,
    chunks,
    src,
    vert,
    win,
    out,
    got1,
    got2,
    got3,
    sum1,
    sum2,
    joined,
    from_core,
    win_send,
    win_recv,
    own_sem,
    send,
    recv,
    far_send,
    far_recv,
):
    me = lax.axis_index("ctx")
    far = devices // 4
    c, x, z = me % 2, (me // 2) % 2, me // 4
    core_peer = me + 1 - 2 * c
    x_peer = me + 2 - 4 * x
    rows = vert.shape[0] // chunks
    half, quarter, piece = rows // 2, rows // 4, rows // devices

    barrier = pltpu.get_barrier_semaphore()

    def greet(k, carry):
        pl.semaphore_signal(
            barrier, inc=1, device_id={"ctx": (me + k) % devices}, device_id_type=MESH
        )
        return carry

    lax.fori_loop(1, devices, greet, 0)
    pl.semaphore_wait(barrier, devices - 1)

    def remote(a, b, s, r, peer):
        return pltpu.make_async_remote_copy(
            src_ref=a, dst_ref=b, send_sem=s, recv_sem=r, device_id={"ctx": peer}, device_id_type=MESH
        )

    def at(ref, start, count):
        return ref.at[pl.ds(pl.multiple_of(start, count), count)]

    def near(k, a, b, peer):
        return remote(a, b, win_send.at[k], win_recv.at[k], peer)

    def stage(s, k):
        base = k * rows
        own_half = base + c * half
        own_quarter = own_half + x * quarter
        own_piece = own_quarter + z * piece
        if s == 0:
            a, b, peer = at(vert, base + (1 - c) * half, half), at(got1, k * half, half), core_peer
        elif s == 1:
            add_rows(sum1, k * half, [(vert, own_half), (got1, k * half)], half)
            a = at(sum1, k * half + (1 - x) * quarter, quarter)
            b, peer = at(got2, k * quarter, quarter), x_peer
        elif s == 2 or s == 3:
            if s == 2:
                add_rows(
                    sum2, k * quarter, [(sum1, k * half + x * quarter), (got2, k * quarter)], quarter
                )
            else:
                add_rows(
                    out,
                    own_piece,
                    [(sum2, k * quarter + z * piece)]
                    + [(got3, (k * (far - 1) + n) * piece) for n in range(far - 1)],
                    piece,
                )
            made = []
            for n in range(1, far):
                peer_z = (z + n) % far
                if s == 2:
                    a = at(sum2, k * quarter + peer_z * piece, piece)
                    b = at(got3, (k * (far - 1) + n - 1) * piece, piece)
                else:
                    a = b = at(out, own_piece, piece)
                made.append(
                    remote(
                        a,
                        b,
                        far_send.at[s - 2, k, n - 1],
                        far_recv.at[s - 2, k, n - 1],
                        peer_z * 4 + me % 4,
                    )
                )
            return made
        elif s == 4:
            a = b = at(out, own_quarter, quarter)
            peer = x_peer
        else:
            a = b = at(out, own_half, half)
            peer = core_peer
        slot = s if s < 2 else s - 2
        return [remote(a, b, send.at[slot, k], recv.at[slot, k], peer)]

    flying = {}
    for k in range(chunks):
        flying[k] = stage(0, k)
        for copy in flying[k]:
            copy.start()
    def joined_rows(n, parts):
        def join(i, carry):
            at_row = pl.ds(pl.multiple_of(i * 16, 16), 16)
            for kind in range(2):
                total = None
                for ref, place, weight in parts:
                    term = ref[place, kind, at_row, :].astype(jnp.float32)
                    term = term if weight is None else term * weight
                    total = term if total is None else total + term
                joined[n, kind, at_row, :] = total.astype(jnp.bfloat16)
            return carry

        lax.fori_loop(0, src.shape[2] // 16, join, 0)

    if back:
        swaps = [
            near(n, src.at[place], from_core.at[n], core_peer)
            for n, place in enumerate((4 - 2 * c, 2 - 2 * c))
        ]
        for copy in swaps:
            copy.start()
        extra = near(2, src.at[4 * c], win.at[2], (me + devices - 5 + 4 * c) % devices)
        extra.start()
        across = near(3, joined.at[0], win.at[0], x_peer)
        along = near(4, joined.at[1], win.at[1], (me + devices - 4) % devices)
        swaps[0].wait()
        joined_rows(0, [(src, WDEV - 2, None), (from_core, 0, None)])
        swaps[1].wait()
    else:
        own = pltpu.make_async_copy(src.at[0], win.at[WDEV], own_sem.at[0])
        own.start()
        along = near(0, src.at[(me + 4) // devices], win.at[WDEV - 4], (me + 4) % devices)
        along.start()
        across = near(1, src.at[0], win.at[WDEV - 2], x_peer)
        passed = near(1, win.at[WDEV - 4], win.at[WDEV - 2], x_peer)
        reach = 1 + 4 * c
        extra = near(2, src.at[(me + reach) // devices], win.at[4 - 4 * c], (me + reach) % devices)
        handed = near(2, win.at[WDEV - 4], win.at[0], (me + 1) % devices)
        late = c * (1 - x)

        @pl.when(x == 0)
        def _():
            across.start()

        @pl.when(late == 0)
        def _():
            extra.start()

        swap_far = near(4, win.at[WDEV - 4], win.at[2 * c], core_peer)
        swap_next = near(3, win.at[WDEV - 2], win.at[2 + 2 * c], core_peer)

    def between(s):
        if back:
            if s == 1:
                across.start()
            elif s == 3:
                across.wait()
                merge = jnp.where(x == 1, 1.0, 0.0).astype(jnp.float32)
                joined_rows(1, [(src, WDEV - 4, None), (from_core, 1, None), (win, 0, merge)])
                along.start()
            elif s == 6:
                along.wait()
                extra.wait()
        elif s == 2:
            along.wait()
            swap_far.start()

            @pl.when(x == 1)
            def _():
                passed.start()

            @pl.when(late == 1)
            def _():
                handed.start()
        elif s == 4:
            across.wait()
            swap_next.start()
        elif s == 6:
            extra.wait()
            swap_far.wait()
            swap_next.wait()
            own.wait()

    for s in range(1, 7):
        for k in range(chunks):
            for copy in flying[k]:
                copy.wait()
            if s < 6:
                flying[k] = stage(s, k)
                for copy in flying[k]:
                    copy.start()
        between(s)


def exchange(src, vert, devices, back):
    rows, dim = vert.shape
    far = devices // 4
    chunks = max(1, min(CHUNKS, rows // (devices * 16)))
    piece = rows // chunks // devices
    slots = 3 if back else WDEV + 1
    slot = (2,) + src.shape[1:] if back else (1, 1, 16, src.shape[3])
    dma = pltpu.SemaphoreType.DMA
    vmem = pl.BlockSpec(memory_space=pltpu.VMEM)
    low = jnp.bfloat16
    return pl.pallas_call(
        functools.partial(exchange_kernel, devices, back, chunks),
        out_shape=(
            jax.ShapeDtypeStruct((slots,) + src.shape[1:], low),
            jax.ShapeDtypeStruct((rows, dim), low),
        ),
        in_specs=[vmem, vmem],
        out_specs=(vmem, vmem),
        scratch_shapes=[
            pltpu.VMEM((rows // 2, dim), low),
            pltpu.VMEM((rows // 4, dim), low),
            pltpu.VMEM((chunks * (far - 1) * piece, dim), low),
            pltpu.VMEM((rows // 2, dim), low),
            pltpu.VMEM((rows // 4, dim), low),
            pltpu.VMEM(slot, low),
            pltpu.VMEM(slot, low),
            dma((5,)),
            dma((5,)),
            dma((1,)),
            dma((4, chunks)),
            dma((4, chunks)),
            dma((2, chunks, far - 1)),
            dma((2, chunks, far - 1)),
        ],
        compiler_params=pltpu.CompilerParams(
            collective_id=1 if back else 0, has_side_effects=True, vmem_limit_bytes=LIMIT
        ),
        name="send_back" if back else "send_out",
    )(src, vert)


def attend_kernel(
    per_device,
    first_ref,
    vert_ref,
    off_ref,
    q_ref,
    g_ref,
    f_ref,
    win_ref,
    vb_ref,
    dq_ref,
    near_ref,
    dvert_ref,
    near,
    dvert,
    w_low,
    s_low,
):
    h = pl.program_id(0)
    dim = vb_ref.shape[3]
    columns = pl.ds(pl.multiple_of(h * dim, dim), dim)
    group = q_ref.shape[1] // dim
    lanes = group * BLOCK
    scaling = 1.0 / math.sqrt(dim)
    near[...] = jnp.zeros_like(near)
    position = lax.broadcasted_iota(jnp.int32, (BLOCK, lanes), 1) % BLOCK
    causal = lax.broadcasted_iota(jnp.int32, (BLOCK, lanes), 0) <= position
    contract_last = (((1,), (1,)), ((), ()))
    contract_first = (((0,), (0,)), ((), ()))
    for j in range(per_device):
        block = first_ref[0] + j

        def stacked(ref):
            return jnp.concatenate(
                [
                    ref[j * BLOCK : (j + 1) * BLOCK, a * dim : (a + 1) * dim]
                    for a in range(group)
                ],
                axis=0,
            )

        q, g, f = stacked(q_ref), stacked(g_ref), stacked(f_ref)
        delta = jnp.sum(
            (g.astype(jnp.float32) * f.astype(jnp.float32)).T, axis=0, keepdims=True
        )
        places, biases = [WDEV * per_device + j], [None]
        for v in range(NV):
            biases.append(jnp.where(vert_ref[h, v] < block, 0.0, NEG))
        for s in range(SLASH_COUNT):
            offset = off_ref[h, s]
            valid = offset > 0
            for v in range(NV):
                valid = valid & (vert_ref[h, v] != block - offset)
            biases.append(jnp.where(valid, 0.0, NEG))
            places.append(WDEV * per_device + j - offset)

        def near_rows(place, kind):
            start = pl.multiple_of((place % per_device) * BLOCK, BLOCK)
            return win_ref[place // per_device, kind, pl.ds(start, BLOCK), columns]

        def candidates(kind):
            return jnp.concatenate(
                [near_rows(places[0], kind)]
                + [vb_ref[v, kind] for v in range(NV)]
                + [near_rows(p, kind) for p in places[1:]],
                axis=0,
            )

        keys, values = candidates(0), candidates(1)
        count = len(biases)
        scores = lax.dot_general(keys, q, contract_last, preferred_element_type=jnp.float32)
        masked = []
        for n in range(count):
            part = scores[n * BLOCK : (n + 1) * BLOCK]
            masked.append(
                jnp.where(causal, part, NEG) if n == 0 else part + biases[n]
            )
        top = masked[0]
        for part in masked[1:]:
            top = jnp.maximum(top, part)
        top = jnp.max(top, axis=0, keepdims=True)
        raised = [jnp.exp((part - top) * scaling) for part in masked]
        total = raised[0]
        for part in raised[1:]:
            total = total + part
        inverse = 1.0 / jnp.sum(total, axis=0, keepdims=True)
        weight_grad = lax.dot_general(
            values, g, contract_last, preferred_element_type=jnp.float32
        )
        for n in range(count):
            rows = slice(n * BLOCK, (n + 1) * BLOCK)
            weights = raised[n] * inverse
            w_low[rows, :] = weights.astype(jnp.bfloat16)
            s_low[rows, :] = (weights * (weight_grad[rows] - delta)).astype(jnp.bfloat16)
        score_low = s_low[...]
        dv = jnp.dot(w_low[...], g, preferred_element_type=jnp.float32)
        dk = jnp.dot(score_low, q, preferred_element_type=jnp.float32) * scaling
        dq = lax.dot_general(keys, score_low, contract_first, preferred_element_type=jnp.float32)
        dq = (dq * scaling).T.astype(jnp.bfloat16)
        for a in range(group):
            dq_ref[j * BLOCK : (j + 1) * BLOCK, a * dim : (a + 1) * dim] = dq[
                a * BLOCK : (a + 1) * BLOCK
            ]
        for kind, grads in enumerate((dk, dv)):
            near[places[0], kind] += grads[:BLOCK]
            for s in range(SLASH_COUNT):
                low = (1 + NV + s) * BLOCK
                near[places[1 + s], kind] += grads[low : low + BLOCK]
            for v in range(NV):
                part = grads[(1 + v) * BLOCK : (2 + v) * BLOCK]
                if j == 0:
                    dvert[v, kind] = part
                else:
                    dvert[v, kind] += part
    for p in range((WDEV + 1) * per_device):
        low = (p % per_device) * BLOCK
        near_ref[p // per_device, :, low : low + BLOCK, columns] = near[p].astype(jnp.bfloat16)
    dvert_ref[...] = dvert[...].astype(jnp.bfloat16)


def gather_kernel(
    per_device, devices, me_ref, slab_ref, vert_ref, near, back, vb, dk, dv
):
    me = me_ref[0]
    slab = slab_ref[0]
    heads = vert_ref.shape[0]
    dim = vb.shape[3]
    outs = (dk, dv)
    step = dk.shape[0]
    g = pl.program_id(0)
    for out in outs:
        out[...] = jnp.zeros_like(out)
    for h in range(heads):
        for v in range(NV):
            block = vert_ref[h, v]
            inner = block % (per_device * devices)

            region = block // (per_device * devices)

            @pl.when((inner // per_device == me) & (region // step == g))
            def _():
                start = pl.multiple_of((inner % per_device) * BLOCK, BLOCK)
                for kind, out in enumerate(outs):
                    out[region % step, pl.ds(start, BLOCK), h * dim : (h + 1) * dim] = vb[
                        h * NV + v, kind
                    ]

    def flag(yes):
        return jnp.where(yes, 1.0, 0.0).astype(jnp.float32)

    far_wraps = me + 4 >= devices
    extra_wraps = me + 1 + 4 * (me % 2) >= devices
    here = [flag((me // 2) % 2 == 0), flag(jnp.logical_not(far_wraps)), flag(jnp.logical_not(extra_wraps))]
    wrapped = [None, flag(far_wraps), flag(extra_wraps)]
    for kind, out in enumerate(outs):

        @pl.when(slab // step == g)
        def _():
            place = slab % step
            current = out[place].astype(jnp.float32) + near[WDEV, kind].astype(jnp.float32)
            for n in range(3):
                current = current + back[n, kind].astype(jnp.float32) * here[n]
            out[place] = current.astype(jnp.bfloat16)

        @pl.when((me + WDEV >= devices) & ((slab - 1) // step == g))
        def _():
            place = (slab - 1) % step
            prior = out[place].astype(jnp.float32)
            for n in range(1, 3):
                prior = prior + back[n, kind].astype(jnp.float32) * wrapped[n]
            out[place] = prior.astype(jnp.bfloat16)


def shards(
    queries,
    context_keys,
    context_values,
    forward_output,
    output_cotangent,
    verticals,
    offsets,
    slab_index,
):
    devices = lax.axis_size("ctx")
    me = lax.axis_index("ctx").astype(jnp.int32)
    row_count, columns = queries.shape
    regions, _, features = context_keys.shape
    heads = verticals.shape[0]
    dim = features // heads
    per_device = row_count // BLOCK
    wide = columns // heads
    smem = pl.BlockSpec(memory_space=pltpu.SMEM)
    vmem = pl.BlockSpec(memory_space=pltpu.VMEM)
    hbm = pl.BlockSpec(memory_space=pltpu.HBM)
    params = pltpu.CompilerParams(vmem_limit_bytes=LIMIT)
    me_arr = me[None]
    low = jnp.bfloat16
    dma = pltpu.SemaphoreType.DMA
    picked, src = pl.pallas_call(
        functools.partial(pick_kernel, per_device, devices),
        out_shape=(
            jax.ShapeDtypeStruct((heads * NV, 2, BLOCK, dim), low),
            jax.ShapeDtypeStruct((2, 2, row_count, features), low),
        ),
        in_specs=[smem, smem, smem, hbm, hbm],
        out_specs=(vmem, vmem),
        scratch_shapes=[dma((heads * NV, 2)), dma((2, 2))],
        compiler_params=pltpu.CompilerParams(vmem_limit_bytes=52 * 1024 * 1024),
        name="pick",
    )(me_arr, slab_index, verticals, context_keys, context_values)
    win, vert = exchange(src, picked.reshape(-1, dim), devices, False)
    first_block = slab_index * (per_device * devices) + me * per_device
    head_rows = pl.BlockSpec((row_count, wide), lambda h, *_: (0, h))
    vert_spec = pl.BlockSpec((NV, 2, BLOCK, dim), lambda h, *_: (h, 0, 0, 0))
    count = 1 + NV + SLASH_COUNT
    lanes = wide // dim * BLOCK
    query_grad, near, vert_grad = pl.pallas_call(
        functools.partial(attend_kernel, per_device),
        out_shape=(
            jax.ShapeDtypeStruct((row_count, columns), low),
            jax.ShapeDtypeStruct((WDEV + 1, 2, row_count, features), low),
            jax.ShapeDtypeStruct((heads * NV, 2, BLOCK, dim), low),
        ),
        grid_spec=pltpu.PrefetchScalarGridSpec(
            num_scalar_prefetch=3,
            grid=(heads,),
            in_specs=[head_rows, head_rows, head_rows, vmem, vert_spec],
            out_specs=(head_rows, vmem, vert_spec),
            scratch_shapes=[
                pltpu.VMEM(((WDEV + 1) * per_device, 2, BLOCK, dim), jnp.float32),
                pltpu.VMEM((NV, 2, BLOCK, dim), jnp.float32),
                pltpu.VMEM((count * BLOCK, lanes), low),
                pltpu.VMEM((count * BLOCK, lanes), low),
            ],
        ),
        compiler_params=pltpu.CompilerParams(vmem_limit_bytes=32 * 1024 * 1024),
        name="attend",
    )(
        first_block,
        verticals,
        offsets,
        queries,
        output_cotangent,
        forward_output,
        win,
        vert.reshape(heads * NV, 2, BLOCK, dim),
    )
    back, vert_sum = exchange(near, vert_grad.reshape(-1, dim), devices, True)
    key_grad, value_grad = pl.pallas_call(
        functools.partial(gather_kernel, per_device, devices),
        out_shape=(
            jax.ShapeDtypeStruct((regions, row_count, features), low),
            jax.ShapeDtypeStruct((regions, row_count, features), low),
        ),
        grid=(4,),
        in_specs=[smem, smem, smem, vmem, vmem, vmem],
        out_specs=(
            pl.BlockSpec((regions // 4, row_count, features), lambda g: (g, 0, 0)),
            pl.BlockSpec((regions // 4, row_count, features), lambda g: (g, 0, 0)),
        ),
        compiler_params=params,
        name="assemble",
    )(
        me_arr,
        slab_index,
        verticals,
        near,
        back,
        vert_sum.reshape(heads * NV, 2, BLOCK, dim),
    )
    return query_grad, key_grad, value_grad


def solution(mesh):
    in_specs = (
        P(("groups", "ctx"), None),
        P("groups", "ctx", None),
        P("groups", "ctx", None),
        P(("groups", "ctx"), None),
        P(("groups", "ctx"), None),
        P("groups", None),
        P("groups", None),
        P("groups"),
    )
    out_specs = (P(("groups", "ctx"), None), P("groups", "ctx", None), P("groups", "ctx", None))
    return jax.shard_map(shards, mesh=mesh, in_specs=in_specs, out_specs=out_specs, check_vma=False)
```
